32 devices in a mesh: seg: 8 (over z, core), bond: 4 (over y, x).
Axes of the slice: x: 2, y: 2, z: 4, core: 2. Of those that a mesh axis runs over, the one named last changes fastest.
Arguments:
- left_env: bfloat16 [8, 1024, 6, 1024], P('seg', 'bond'), may hold values from -0.1875 to 0.1875
- prev_left: bfloat16 [8, 1024, 1024], P('seg'), may hold values from -0.25 to 1.25
- cur_site: bfloat16 [8, 1024, 4, 1024], P('seg', 'bond'), may hold values from -6 to 6
- prev_site: bfloat16 [8, 1024, 4, 1024], P('seg', None, None, 'bond'), may hold values from -6 to 6
- hamiltonian: bfloat16 [8, 6, 6, 4, 4], P('seg'), may hold values from -1.25 to 1.25
- right_env: bfloat16 [8, 1024, 6, 1024], P('seg', 'bond'), may hold values from -0.078125 to 0.078125
- prev_right: bfloat16 [8, 1024, 1024], P('seg'), may hold values from -0.25 to 1.25
Outputs:
- new_site: bfloat16 [8, 1024, 4, 1024], P('seg', 'bond')
- center: float32 [8, 1024, 1024], P('seg', 'bond')
The draws below stay inside these ranges and needn't reach their ends.
All inputs are finite; a program needn't handle non-finite values.
Results may differ from the reference program's by a relative error of at most 0.0054.
Values may be sent and summed in bfloat16 or wider, within the bound.
A program may use at most 128 MiB of HBM per device.

```python
import math
import jax
import jax.numpy as jnp
from jax import lax

CHI = 1024
PHYS = 4
MPOB = 6
SEGMENTS = 8


def dominant_square(key):
    noise = jax.random.normal(key, (SEGMENTS, CHI, CHI), jnp.float32)
    noise = jnp.clip(noise * (0.5 / math.sqrt(CHI)), -0.25, 0.25)
    return noise + jnp.eye(CHI, dtype=jnp.float32)[None]


def draw_prev_left(key, part):
    return dominant_square(jax.random.fold_in(key, 11)).astype(jnp.bfloat16)


def draw_prev_right(key, part):
    return dominant_square(jax.random.fold_in(key, 23)).astype(jnp.bfloat16)


def draw_prev_site(key, part):
    first = jax.random.fold_in(key, 37)
    base = jax.random.normal(first, (SEGMENTS, CHI, PHYS, CHI), jnp.float32)
    return jnp.clip(base, -6.0, 6.0).astype(jnp.bfloat16)


def block_levels(rng, extent, cuts, low, top_value):
    level, own = 1.0, jax.random.fold_in(rng, 6)
    for position, parts in cuts:
        heights = jnp.exp(jax.random.uniform(jax.random.fold_in(own, position), (parts,), jnp.float32, low / len(cuts), top_value / len(cuts)))
        level = level * jnp.repeat(heights, extent[position] // parts).reshape([-1 if axis == position else 1 for axis in range(len(extent))])
    return level


def gaussian(stream_key, dims, deviation, most, split=(), kind=jnp.bfloat16):
    values = jax.random.normal(stream_key, dims, jnp.float32) * deviation
    if len(split) > 0:
        values = block_levels(stream_key, dims, split, -0.22, 0.18) * values
    return jnp.clip(values, min=-most, max=most).astype(kind)


def setup_inputs(seed: int = 0) -> dict:
    streams_of = jax.random.split(jax.random.key(seed), 8)
    return {
        "left_env": gaussian(streams_of[0], (SEGMENTS, CHI, MPOB, CHI), CHI ** -0.5, 0.1875, ((0, 8), (1, 4))),
        "prev_left": draw_prev_left(jax.random.fold_in(streams_of[7], 71), 0),
        "cur_site": gaussian(streams_of[2], (SEGMENTS, CHI, PHYS, CHI), 1.0, 6.0, ((0, 8), (1, 4))),
        "prev_site": draw_prev_site(jax.random.fold_in(streams_of[7], 71), 0),
        "hamiltonian": gaussian(streams_of[4], (SEGMENTS, MPOB, MPOB, PHYS, PHYS), (MPOB * PHYS) ** -0.5, 1.25, ((0, 8),)),
        "right_env": gaussian(streams_of[5], (SEGMENTS, CHI, MPOB, CHI), (MPOB * CHI) ** -0.5, 0.078125, ((0, 8), (1, 4))),
        "prev_right": draw_prev_right(jax.random.fold_in(streams_of[7], 71), 0),
    }


def segment_step(pieces):
    left_now, prev_now, current, previous, hamiltonian, right_block, prev_block = pieces
    projected = jnp.dot(left_now.reshape(CHI * MPOB, CHI).astype(jnp.float32), current.reshape(CHI, PHYS * CHI).astype(jnp.float32), preferred_element_type=jnp.float32).reshape(CHI, MPOB, PHYS, CHI)
    mixture = jnp.einsum('autc,uvst->asvc', projected, hamiltonian.astype(jnp.float32), precision=lax.Precision.HIGHEST).astype(jnp.bfloat16)
    right_flat = jnp.transpose(right_block, (1, 0, 2)).reshape(MPOB * CHI, CHI)
    applied = jnp.dot(mixture.reshape(CHI * PHYS, MPOB * CHI).astype(jnp.float32), right_flat.astype(jnp.float32), preferred_element_type=jnp.float32)
    partial_value = jnp.dot(prev_now.astype(jnp.float32), previous.reshape(CHI, PHYS * CHI).astype(jnp.float32), preferred_element_type=jnp.float32).astype(jnp.bfloat16)
    second = jnp.dot(partial_value.reshape(CHI * PHYS, CHI).astype(jnp.float32), prev_block.astype(jnp.float32), preferred_element_type=jnp.float32)
    target = 2.0 * applied - second
    correlation = jnp.dot(target.T.astype(jnp.float32), target.astype(jnp.float32), precision=lax.Precision.HIGHEST, preferred_element_type=jnp.float32)
    triangle = jnp.linalg.cholesky(correlation)
    solved = jax.scipy.linalg.solve_triangular(triangle, target.T, lower=True)
    norming = math.sqrt(CHI * PHYS)
    new_site = (solved.T * norming).astype(jnp.bfloat16).reshape(CHI, PHYS, CHI)
    center = triangle.T / norming
    return (new_site, center)

def reference(left_env, prev_left, cur_site, prev_site, hamiltonian, right_env, prev_right):
    left_now = jnp.roll(left_env, 1, axis=0)
    prev_now = jnp.roll(prev_left, 1, axis=0)
    new_site, center = lax.map(segment_step, (left_now, prev_now, cur_site, prev_site, hamiltonian, right_env, prev_right))
    return (new_site, center)
```

```python
import math

import jax
import jax.numpy as jnp
from jax import lax
from jax.experimental import pallas as pl
from jax.experimental.pallas import tpu as pltpu
from jax.sharding import PartitionSpec as P

PHYS = 4
MPOB = 6
BLOCK = 128
STRIP = 256
GROUP = 4


def shifted(block, axis, distance):
    devices = range(lax.axis_size(axis))
    route = [((i - distance) % len(devices), i) for i in devices]
    return lax.ppermute(block, axis, route)


def halves(x):
    high = x.astype(jnp.bfloat16)
    return high, (x - high.astype(jnp.float32)).astype(jnp.bfloat16)


def product(a, b, dims):
    a_high, a_low = halves(a)
    b_high, b_low = halves(b)

    def dot(x, y):
        return lax.dot_general(x, y, (dims, ((), ())), preferred_element_type=jnp.float32)

    return dot(a_high, b_high) + (dot(a_high, b_low) + dot(a_low, b_high))


def eliminate(block, rows_ref):
    size = block.shape[0]
    lane = lax.broadcasted_iota(jnp.int32, (1, size), 1)
    rest = block
    top = 0
    for first in range(0, size, GROUP):
        start = first // 8 * 8
        rest, top = rest[start - top :], start
        at = first - top
        rows = [rest[at + q : at + q + 1, :] for q in range(GROUP)]
        columns = [
            jnp.broadcast_to(rest[:, first + q : first + q + 1], rest.shape) for q in range(GROUP)
        ]
        small = [[columns[r][at + p : at + p + 1, :] for r in range(GROUP)] for p in range(GROUP)]
        change = None
        for q in range(GROUP):
            rows_ref[pl.ds(first + q, 1), :] = rows[q]
            inverse = 1.0 / small[q][q]
            lead = jnp.where(lane == first + q, 1.0, rows[q])
            for p in range(q + 1, GROUP):
                factor = small[q][p] * inverse
                for r in range(p, GROUP):
                    small[p][r] = small[p][r] - factor * small[q][r]
                rows[p] = jnp.where(lane == first + q, 0.0, rows[p]) - factor * lead
                columns[p] = columns[p] - factor * columns[q]
            if first + GROUP < size:
                lead = jnp.where((lane > first + q) & (lane < first + GROUP), 0.0, lead)
                term = columns[q] * (inverse * lead)
                change = term if change is None else change + term
        if first + GROUP < size:
            rest = jnp.where((lane >= first) & (lane < first + GROUP), 0.0, rest) - change


def factor_kernel(packed_ref, upper_ref, inverse_ref, work, panel, rows_ref):
    size = work.shape[0]
    blocks = size // BLOCK
    offset = 0
    for start in range(0, size, STRIP):
        width = size - start
        work[start : start + STRIP, start:] = packed_ref[:, offset : offset + width]
        if start > 0:
            work[start : start + STRIP, :start] = jnp.zeros((STRIP, start), jnp.float32)
        offset += width
    row = lax.broadcasted_iota(jnp.int32, (BLOCK, BLOCK), 0)
    column = lax.broadcasted_iota(jnp.int32, (BLOCK, BLOCK), 1)
    full_column = lax.broadcasted_iota(jnp.int32, (BLOCK, size), 1)

    def step(k, carry):
        own = pl.ds(pl.multiple_of(k * BLOCK, BLOCK), BLOCK)
        eliminate(work[own, own], rows_ref)
        done = rows_ref[...]
        pivots = jnp.sum(jnp.where(row == column, done, 0.0), axis=1, keepdims=True)
        scale = lax.rsqrt(pivots)
        scaled = done * scale
        upper = jnp.where(row <= column, scaled, 0.0)
        inverse = jnp.where(row > column, scaled, jnp.where(row == column, scale, 0.0))
        panel[...] = product(inverse, work[own, :], ((1,), (0,)))
        whole = panel[...]
        upper_ref[own, :] = jnp.where(full_column >= (k + 1) * BLOCK, whole, 0.0)
        inverse_ref[own, :] = jnp.where(full_column < k * BLOCK, whole, 0.0)
        upper_ref[own, own] = upper
        inverse_ref[own, own] = inverse
        panel[:, own] = inverse
        right = panel[...]

        def update(i, carry):
            other = pl.ds(pl.multiple_of(i * BLOCK, BLOCK), BLOCK)
            work[other, own] = jnp.zeros((BLOCK, BLOCK), jnp.float32)
            work[other, :] -= product(panel[:, other], right, ((0,), (0,)))
            return carry

        lax.fori_loop(k + 1, blocks, update, 0)
        return carry

    lax.fori_loop(0, blocks, step, 0)


def factorize(packed, size):
    whole = jax.ShapeDtypeStruct((size, size), jnp.float32)
    return pl.pallas_call(
        factor_kernel,
        out_shape=(whole, whole),
        in_specs=[pl.BlockSpec(memory_space=pltpu.VMEM)],
        out_specs=[pl.BlockSpec(memory_space=pltpu.VMEM)] * 2,
        scratch_shapes=[
            pltpu.VMEM((size, size), jnp.float32),
            pltpu.VMEM((BLOCK, size), jnp.float32),
            pltpu.VMEM((BLOCK, BLOCK), jnp.float32),
        ],
        compiler_params=pltpu.CompilerParams(vmem_limit_bytes=40 * 2**20),
        name="factorize",
    )(packed)


def shards(left_env, prev_left, cur_site, prev_site, hamiltonian, right_env, prev_right):
    left_now, prev_now = shifted((left_env[0], prev_left[0]), "seg", 1)
    own_rows = left_now.shape[0]
    bond_width = left_now.shape[2]
    coupling = hamiltonian[0].astype(jnp.float32)
    current = lax.all_gather(cur_site[0], "bond", axis=0, tiled=True)
    projected = jnp.dot(
        left_now.reshape(own_rows * MPOB, bond_width),
        current.reshape(bond_width, PHYS * bond_width),
        preferred_element_type=jnp.float32,
    ).reshape(own_rows, MPOB, PHYS, bond_width)
    mixture = jnp.einsum(
        "autc,uvst->asvc", projected, coupling, precision=lax.Precision.HIGH
    ).astype(jnp.bfloat16)
    applied = jnp.einsum(
        "asvc,cvy->asy",
        mixture,
        lax.all_gather(right_env[0], "bond", axis=0, tiled=True),
        preferred_element_type=jnp.float32,
    )
    partial_value = jnp.einsum(
        "ab,bsc->asc", prev_now, prev_site[0], preferred_element_type=jnp.float32
    ).astype(jnp.bfloat16)
    second = jnp.einsum(
        "akc,cy->aky",
        lax.all_to_all(partial_value, "bond", split_axis=0, concat_axis=2, tiled=True),
        prev_right[0],
        preferred_element_type=jnp.float32,
    )
    target = (2.0 * applied - second).reshape(own_rows * PHYS, bond_width)
    strips = [
        jnp.dot(
            target[:, start : start + STRIP].T,
            target[:, start:],
            precision=lax.Precision.HIGH,
            preferred_element_type=jnp.float32,
        )
        for start in range(0, bond_width, STRIP)
    ]
    packed = lax.psum(jnp.concatenate(strips, axis=1), "bond")
    upper, inverse = factorize(packed, bond_width)
    norming = math.sqrt(bond_width * PHYS)
    solved = lax.dot_general(
        target,
        inverse,
        (((1,), (1,)), ((), ())),
        precision=lax.Precision.HIGH,
        preferred_element_type=jnp.float32,
    )
    new_site = (solved * norming).astype(jnp.bfloat16).reshape(1, own_rows, PHYS, bond_width)
    offset = lax.axis_index("bond") * own_rows
    center = lax.dynamic_slice_in_dim(upper, offset, own_rows, 0) / norming
    return (new_site, center[None])


def solution(mesh):
    return jax.shard_map(
        shards,
        mesh=mesh,
        in_specs=(
            P("seg", "bond", None, None),
            P("seg", None, None),
            P("seg", "bond", None, None),
            P("seg", None, None, "bond"),
            P("seg", None, None, None, None),
            P("seg", "bond", None, None),
            P("seg", None, None),
        ),
        out_specs=(P("seg", "bond", None, None), P("seg", "bond", None)),
        check_vma=False,
    )
```

```python
import functools
import math

import jax
import jax.numpy as jnp
from jax import lax
from jax.experimental import pallas as pl
from jax.experimental.pallas import tpu as pltpu
from jax.sharding import PartitionSpec as P

PHYS = 4
MPOB = 6
BLOCK = 128
STRIP = 256
GROUP = 4
TERMS = 2
ROWS = 8
WAVES = 2


def shifted(block, axis, distance):
    devices = range(lax.axis_size(axis))
    route = [((i - distance) % len(devices), i) for i in devices]
    return lax.ppermute(block, axis, route)


def halves(x):
    high = x.astype(jnp.bfloat16)
    return high, (x - high.astype(jnp.float32)).astype(jnp.bfloat16)


def product(a, b, dims):
    a_high, a_low = halves(a)
    b_high, b_low = halves(b)

    def dot(x, y):
        return lax.dot_general(x, y, (dims, ((), ())), preferred_element_type=jnp.float32)

    return dot(a_high, b_high) + (dot(a_high, b_low) + dot(a_low, b_high))


def reduce_kernel(n, own_ref, out_ref, parts, total, send_sem, recv_sem, send_back, recv_back):
    me = lax.axis_index("bond")
    barrier = pltpu.get_barrier_semaphore()
    peers = [lax.rem(me + d, n) for d in range(1, n)]
    for peer in peers:
        pl.semaphore_signal(barrier, inc=1, device_id={"bond": peer})
    pl.semaphore_wait(barrier, n - 1)
    width = own_ref.shape[2] // WAVES
    waves = [pl.ds(w * width, width) for w in range(WAVES)]
    outward, back = [], []
    for w, lanes in enumerate(waves):
        outward.append([
            pltpu.make_async_remote_copy(
                src_ref=own_ref.at[peer, :, lanes],
                dst_ref=parts.at[d, :, lanes],
                send_sem=send_sem.at[w, d],
                recv_sem=recv_sem.at[w, d],
                device_id={"bond": peer},
            )
            for d, peer in enumerate(peers)
        ])
        for copy in outward[w]:
            copy.start()
    for w, lanes in enumerate(waves):
        for copy in outward[w]:
            copy.wait_recv()
        value = own_ref[me, :, lanes]
        for d in range(n - 1):
            value = value + parts[d, :, lanes]
        total[me, :, lanes] = value
        back.append([
            pltpu.make_async_remote_copy(
                src_ref=total.at[me, :, lanes],
                dst_ref=total.at[me, :, lanes],
                send_sem=send_back.at[w, d],
                recv_sem=recv_back.at[w, d],
                device_id={"bond": peer},
            )
            for d, peer in enumerate(peers)
        ])
        for copy in back[w]:
            copy.start()
    for w, lanes in enumerate(waves):
        for copy in back[w]:
            copy.wait_recv()
        out_ref[:, :, lanes] = total[:, :, lanes]
    for copies in outward + back:
        for copy in copies:
            copy.wait_send()


def summed(packed):
    n = lax.axis_size("bond")
    rows, width = packed.shape
    shape = (n, rows // n, width)
    return pl.pallas_call(
        functools.partial(reduce_kernel, n),
        out_shape=jax.ShapeDtypeStruct(shape, jnp.float32),
        in_specs=[pl.BlockSpec(memory_space=pltpu.VMEM)],
        out_specs=pl.BlockSpec(memory_space=pltpu.VMEM),
        scratch_shapes=[
            pltpu.VMEM((n - 1,) + shape[1:], jnp.float32),
            pltpu.VMEM(shape, jnp.float32),
        ]
        + [pltpu.SemaphoreType.DMA((WAVES, n - 1))] * 4,
        compiler_params=pltpu.CompilerParams(
            collective_id=0, has_side_effects=True, vmem_limit_bytes=24 * 2**20
        ),
        name="summed",
    )(packed.reshape(shape)).reshape(rows, width)


def eliminate(block, rows_ref):
    size = block.shape[0]
    lane = lax.broadcasted_iota(jnp.int32, (1, size), 1)
    rest = block
    top = 0
    for first in range(0, size, GROUP):
        start = first // 8 * 8
        rest, top = rest[start - top :], start
        at = first - top
        rows = [rest[at + q : at + q + 1, :] for q in range(GROUP)]
        columns = [
            jnp.broadcast_to(rest[:, first + q : first + q + 1], rest.shape) for q in range(GROUP)
        ]
        small = [[columns[r][at + p : at + p + 1, :] for r in range(GROUP)] for p in range(GROUP)]
        change = None
        for q in range(GROUP):
            rows_ref[pl.ds(first + q, 1), :] = rows[q]
            inverse = 1.0 / small[q][q]
            lead = jnp.where(lane == first + q, 1.0, rows[q])
            for p in range(q + 1, GROUP):
                factor = small[q][p] * inverse
                for r in range(p, GROUP):
                    small[p][r] = small[p][r] - factor * small[q][r]
                rows[p] = jnp.where(lane == first + q, 0.0, rows[p]) - factor * lead
                columns[p] = columns[p] - factor * columns[q]
            if first + GROUP < size:
                lead = jnp.where((lane > first + q) & (lane < first + GROUP), 0.0, lead)
                term = columns[q] * (inverse * lead)
                change = term if change is None else change + term
        if first + GROUP < size:
            rest = jnp.where((lane >= first) & (lane < first + GROUP), 0.0, rest) - change


def factor_kernel(packed_ref, upper_ref, inverse_ref, work, panel, rows_ref):
    size = work.shape[0]
    blocks = size // BLOCK
    offset = 0
    for start in range(0, size, STRIP):
        width = size - start
        work[start : start + STRIP, start:] = packed_ref[:, offset : offset + width]
        if start > 0:
            work[start : start + STRIP, :start] = jnp.zeros((STRIP, start), jnp.float32)
        offset += width
    row = lax.broadcasted_iota(jnp.int32, (BLOCK, BLOCK), 0)
    column = lax.broadcasted_iota(jnp.int32, (BLOCK, BLOCK), 1)
    full_column = lax.broadcasted_iota(jnp.int32, (BLOCK, size), 1)

    def step(k, carry):
        own = pl.ds(pl.multiple_of(k * BLOCK, BLOCK), BLOCK)
        eliminate(work[own, own], rows_ref)
        done = rows_ref[...]
        pivots = jnp.sum(jnp.where(row == column, done, 0.0), axis=1, keepdims=True)
        scale = lax.rsqrt(pivots)
        scaled = done * scale
        upper = jnp.where(row <= column, scaled, 0.0)
        inverse = jnp.where(row > column, scaled, jnp.where(row == column, scale, 0.0))
        panel[...] = product(inverse, work[own, :], ((1,), (0,)))
        whole = panel[...]
        upper_ref[own, :] = jnp.where(full_column >= (k + 1) * BLOCK, whole, 0.0)
        inverse_ref[own, :] = jnp.where(full_column < k * BLOCK, whole, 0.0)
        upper_ref[own, own] = upper
        inverse_ref[own, own] = inverse
        panel[:, own] = inverse
        right = panel[...]

        def update(i, carry):
            other = pl.ds(pl.multiple_of(i * BLOCK, BLOCK), BLOCK)
            work[other, own] = jnp.zeros((BLOCK, BLOCK), jnp.float32)
            work[other, :] -= product(panel[:, other], right, ((0,), (0,)))
            return carry

        lax.fori_loop(k + 1, blocks, update, 0)
        return carry

    lax.fori_loop(0, blocks, step, 0)


def factorize(packed, size):
    whole = jax.ShapeDtypeStruct((size, size), jnp.float32)
    return pl.pallas_call(
        factor_kernel,
        out_shape=(whole, whole),
        in_specs=[pl.BlockSpec(memory_space=pltpu.VMEM)],
        out_specs=[pl.BlockSpec(memory_space=pltpu.VMEM)] * 2,
        scratch_shapes=[
            pltpu.VMEM((size, size), jnp.float32),
            pltpu.VMEM((BLOCK, size), jnp.float32),
            pltpu.VMEM((BLOCK, BLOCK), jnp.float32),
        ],
        compiler_params=pltpu.CompilerParams(vmem_limit_bytes=40 * 2**20),
        name="factorize",
    )(packed)


def mix_kernel(spread_ref, projected_ref, mixture_ref):
    width = projected_ref.shape[2] // PHYS
    spread = spread_ref[...]
    results = []
    for first in range(0, 2 * ROWS, ROWS):
        stack = jnp.concatenate(
            [
                projected_ref[u, first : first + ROWS, t * width : (t + 1) * width]
                for u in range(MPOB)
                for t in range(PHYS)
            ],
            axis=0,
        )
        high, low = halves(stack)
        results.append(
            jnp.dot(spread, high, preferred_element_type=jnp.float32)
            + jnp.dot(spread, low, preferred_element_type=jnp.float32)
        )
    for v in range(MPOB):
        for s in range(PHYS):
            at = (v * PHYS + s) * ROWS
            both = jnp.concatenate([part[at : at + ROWS, :] for part in results], axis=0)
            mixture_ref[v, s] = both.astype(jnp.bfloat16)


def mixed(projected, coupling):
    own_rows, width = projected.shape[1], projected.shape[2] // PHYS
    side = MPOB * PHYS * ROWS
    diagonal = jnp.eye(ROWS, dtype=coupling.dtype)
    turned = jnp.transpose(coupling, (1, 2, 0, 3))
    spread = turned[:, :, None, :, :, None] * diagonal[None, None, :, None, None, :]
    return pl.pallas_call(
        mix_kernel,
        grid=(own_rows // (2 * ROWS),),
        out_shape=jax.ShapeDtypeStruct((MPOB, PHYS, own_rows, width), jnp.bfloat16),
        in_specs=[
            pl.BlockSpec((side, side), lambda i: (0, 0)),
            pl.BlockSpec((MPOB, 2 * ROWS, PHYS * width), lambda i: (0, i, 0)),
        ],
        out_specs=pl.BlockSpec((MPOB, PHYS, 2 * ROWS, width), lambda i: (0, 0, i, 0)),
        compiler_params=pltpu.CompilerParams(vmem_limit_bytes=40 * 2**20),
        cost_estimate=pl.CostEstimate(
            flops=4 * side * MPOB * PHYS * own_rows * width,
            bytes_accessed=6 * MPOB * PHYS * own_rows * width,
            transcendentals=0,
        ),
        name="mixed",
    )(spread.reshape(side, side), projected)


def shards(left_env, prev_left, cur_site, prev_site, hamiltonian, right_env, prev_right):
    left_now, prev_now = shifted((left_env[0], prev_left[0]), "seg", 1)
    own_rows = left_now.shape[0]
    bond_width = left_now.shape[2]
    current = lax.all_gather(cur_site[0], "bond", axis=0, tiled=True)
    left_terms = jnp.transpose(left_now, (1, 0, 2)).reshape(MPOB * own_rows, bond_width)
    projected = jnp.dot(
        left_terms,
        current.reshape(bond_width, PHYS * bond_width),
        preferred_element_type=jnp.float32,
    ).reshape(MPOB, own_rows, PHYS * bond_width)
    mixture = mixed(projected, hamiltonian[0])
    partial_value = jnp.einsum(
        "ab,bsc->asc", prev_now, prev_site[0], preferred_element_type=jnp.float32
    ).astype(jnp.bfloat16)
    second = jnp.einsum(
        "akc,cy->kay",
        lax.all_to_all(partial_value, "bond", split_axis=0, concat_axis=2, tiled=True),
        prev_right[0],
        preferred_element_type=jnp.float32,
    )
    flat_rows = own_rows * PHYS
    right_terms = jnp.transpose(right_env[0], (1, 0, 2))
    applied = 0.0
    for start in range(0, MPOB, TERMS):
        right = lax.all_gather(right_terms[start : start + TERMS], "bond", axis=1, tiled=True)
        for v in range(TERMS):
            applied += jnp.dot(
                mixture[start + v].reshape(flat_rows, bond_width),
                right[v],
                preferred_element_type=jnp.float32,
            )
    target = 2.0 * applied - second.reshape(flat_rows, bond_width)
    strips = [
        jnp.dot(
            target[:, start : start + STRIP].T,
            target[:, start:],
            precision=lax.Precision.HIGH,
            preferred_element_type=jnp.float32,
        )
        for start in range(0, bond_width, STRIP)
    ]
    packed = summed(jnp.concatenate(strips, axis=1))
    upper, inverse = factorize(packed, bond_width)
    norming = math.sqrt(bond_width * PHYS)
    solved = lax.dot_general(
        target,
        inverse,
        (((1,), (1,)), ((), ())),
        precision=lax.Precision.HIGH,
        preferred_element_type=jnp.float32,
    )
    new_site = (solved * norming).astype(jnp.bfloat16).reshape(PHYS, own_rows, bond_width)
    new_site = jnp.transpose(new_site, (1, 0, 2))[None]
    offset = lax.axis_index("bond") * own_rows
    center = lax.dynamic_slice_in_dim(upper, offset, own_rows, 0) / norming
    return (new_site, center[None])


def solution(mesh):
    return jax.shard_map(
        shards,
        mesh=mesh,
        in_specs=(
            P("seg", "bond", None, None),
            P("seg", None, None),
            P("seg", "bond", None, None),
            P("seg", None, None, "bond"),
            P("seg", None, None, None, None),
            P("seg", "bond", None, None),
            P("seg", None, None),
        ),
        out_specs=(P("seg", "bond", None, None), P("seg", "bond", None)),
        check_vma=False,
    )
```

```python
import functools
import math

import jax
import jax.numpy as jnp
from jax import lax
from jax.experimental import pallas as pl
from jax.experimental.pallas import tpu as pltpu
from jax.sharding import PartitionSpec as P

PHYS = 4
MPOB = 6
BLOCK = 128
STRIP = 256
GROUP = 4
ROWS = 8
WAVES = 2


def shifted(block, axis, distance):
    devices = range(lax.axis_size(axis))
    route = [((i - distance) % len(devices), i) for i in devices]
    return lax.ppermute(block, axis, route)


def halves(x):
    high = x.astype(jnp.bfloat16)
    return high, (x - high.astype(jnp.float32)).astype(jnp.bfloat16)


def product(a, b, dims):
    a_high, a_low = halves(a)
    b_high, b_low = halves(b)

    def dot(x, y):
        return lax.dot_general(x, y, (dims, ((), ())), preferred_element_type=jnp.float32)

    return dot(a_high, b_high) + (dot(a_high, b_low) + dot(a_low, b_high))


def reduce_kernel(n, own_ref, out_ref, parts, total, send_sem, recv_sem, send_back, recv_back):
    me = lax.axis_index("bond")
    barrier = pltpu.get_barrier_semaphore()
    peers = [lax.rem(me + d, n) for d in range(1, n)]
    for peer in peers:
        pl.semaphore_signal(barrier, inc=1, device_id={"bond": peer})
    pl.semaphore_wait(barrier, n - 1)
    width = own_ref.shape[2] // WAVES
    waves = [pl.ds(w * width, width) for w in range(WAVES)]
    outward, back = [], []
    for w, lanes in enumerate(waves):
        outward.append([
            pltpu.make_async_remote_copy(
                src_ref=own_ref.at[peer, :, lanes],
                dst_ref=parts.at[d, :, lanes],
                send_sem=send_sem.at[w, d],
                recv_sem=recv_sem.at[w, d],
                device_id={"bond": peer},
            )
            for d, peer in enumerate(peers)
        ])
        for copy in outward[w]:
            copy.start()
    for w, lanes in enumerate(waves):
        for copy in outward[w]:
            copy.wait_recv()
        value = own_ref[me, :, lanes]
        for d in range(n - 1):
            value = value + parts[d, :, lanes]
        total[me, :, lanes] = value
        back.append([
            pltpu.make_async_remote_copy(
                src_ref=total.at[me, :, lanes],
                dst_ref=total.at[me, :, lanes],
                send_sem=send_back.at[w, d],
                recv_sem=recv_back.at[w, d],
                device_id={"bond": peer},
            )
            for d, peer in enumerate(peers)
        ])
        for copy in back[w]:
            copy.start()
    for w, lanes in enumerate(waves):
        for copy in back[w]:
            copy.wait_recv()
        out_ref[:, :, lanes] = total[:, :, lanes]
    for copies in outward + back:
        for copy in copies:
            copy.wait_send()


def summed(packed):
    n = lax.axis_size("bond")
    rows, width = packed.shape
    shape = (n, rows // n, width)
    return pl.pallas_call(
        functools.partial(reduce_kernel, n),
        out_shape=jax.ShapeDtypeStruct(shape, jnp.float32),
        in_specs=[pl.BlockSpec(memory_space=pltpu.VMEM)],
        out_specs=pl.BlockSpec(memory_space=pltpu.VMEM),
        scratch_shapes=[
            pltpu.VMEM((n - 1,) + shape[1:], jnp.float32),
            pltpu.VMEM(shape, jnp.float32),
        ]
        + [pltpu.SemaphoreType.DMA((WAVES, n - 1))] * 4,
        compiler_params=pltpu.CompilerParams(
            collective_id=0, has_side_effects=True, vmem_limit_bytes=24 * 2**20
        ),
        name="summed",
    )(packed.reshape(shape)).reshape(rows, width)


def eliminate(block, rows_ref):
    size = block.shape[0]
    lane = lax.broadcasted_iota(jnp.int32, (1, size), 1)
    rest = block
    top = 0
    for first in range(0, size, GROUP):
        start = first // 8 * 8
        rest, top = rest[start - top :], start
        at = first - top
        rows = [rest[at + q : at + q + 1, :] for q in range(GROUP)]
        columns = [
            jnp.broadcast_to(rest[:, first + q : first + q + 1], rest.shape) for q in range(GROUP)
        ]
        small = [[columns[r][at + p : at + p + 1, :] for r in range(GROUP)] for p in range(GROUP)]
        change = None
        for q in range(GROUP):
            rows_ref[pl.ds(first + q, 1), :] = rows[q]
            inverse = 1.0 / small[q][q]
            lead = jnp.where(lane == first + q, 1.0, rows[q])
            for p in range(q + 1, GROUP):
                factor = small[q][p] * inverse
                for r in range(p, GROUP):
                    small[p][r] = small[p][r] - factor * small[q][r]
                rows[p] = jnp.where(lane == first + q, 0.0, rows[p]) - factor * lead
                columns[p] = columns[p] - factor * columns[q]
            if first + GROUP < size:
                lead = jnp.where((lane > first + q) & (lane < first + GROUP), 0.0, lead)
                term = columns[q] * (inverse * lead)
                change = term if change is None else change + term
        if first + GROUP < size:
            rest = jnp.where((lane >= first) & (lane < first + GROUP), 0.0, rest) - change


def factor_kernel(packed_ref, upper_ref, inverse_ref, work, panel, rows_ref):
    size = work.shape[0]
    blocks = size // BLOCK
    offset = 0
    for start in range(0, size, STRIP):
        width = size - start
        work[start : start + STRIP, start:] = packed_ref[:, offset : offset + width]
        if start > 0:
            work[start : start + STRIP, :start] = jnp.zeros((STRIP, start), jnp.float32)
        offset += width
    row = lax.broadcasted_iota(jnp.int32, (BLOCK, BLOCK), 0)
    column = lax.broadcasted_iota(jnp.int32, (BLOCK, BLOCK), 1)
    full_column = lax.broadcasted_iota(jnp.int32, (BLOCK, size), 1)

    def step(k, carry):
        own = pl.ds(pl.multiple_of(k * BLOCK, BLOCK), BLOCK)
        eliminate(work[own, own], rows_ref)
        done = rows_ref[...]
        pivots = jnp.sum(jnp.where(row == column, done, 0.0), axis=1, keepdims=True)
        scale = lax.rsqrt(pivots)
        scaled = done * scale
        upper = jnp.where(row <= column, scaled, 0.0)
        inverse = jnp.where(row > column, scaled, jnp.where(row == column, scale, 0.0))
        panel[...] = product(inverse, work[own, :], ((1,), (0,)))
        whole = panel[...]
        upper_ref[own, :] = jnp.where(full_column >= (k + 1) * BLOCK, whole, 0.0)
        inverse_ref[own, :] = jnp.where(full_column < k * BLOCK, whole, 0.0)
        upper_ref[own, own] = upper
        inverse_ref[own, own] = inverse
        panel[:, own] = inverse
        right = panel[...]

        def update(i, carry):
            other = pl.ds(pl.multiple_of(i * BLOCK, BLOCK), BLOCK)
            work[other, own] = jnp.zeros((BLOCK, BLOCK), jnp.float32)
            work[other, :] -= product(panel[:, other], right, ((0,), (0,)))
            return carry

        lax.fori_loop(k + 1, blocks, update, 0)
        return carry

    lax.fori_loop(0, blocks, step, 0)


def factorize(packed, size):
    whole = jax.ShapeDtypeStruct((size, size), jnp.float32)
    return pl.pallas_call(
        factor_kernel,
        out_shape=(whole, whole),
        in_specs=[pl.BlockSpec(memory_space=pltpu.VMEM)],
        out_specs=[pl.BlockSpec(memory_space=pltpu.VMEM)] * 2,
        scratch_shapes=[
            pltpu.VMEM((size, size), jnp.float32),
            pltpu.VMEM((BLOCK, size), jnp.float32),
            pltpu.VMEM((BLOCK, BLOCK), jnp.float32),
        ],
        compiler_params=pltpu.CompilerParams(vmem_limit_bytes=40 * 2**20),
        name="factorize",
    )(packed)


def mix_kernel(parts, spread_ref, projected_ref, mixture_ref):
    width = projected_ref.shape[2] // PHYS
    spread = spread_ref[...]
    results = []
    for first in range(0, 2 * ROWS, ROWS):
        stack = jnp.concatenate(
            [
                projected_ref[u, first : first + ROWS, t * width : (t + 1) * width]
                for u in range(MPOB)
                for t in range(PHYS)
            ],
            axis=0,
        )
        high, low = halves(stack)
        results.append(
            jnp.dot(spread, high, preferred_element_type=jnp.float32)
            + jnp.dot(spread, low, preferred_element_type=jnp.float32)
        )
    for v in range(MPOB):
        for s in range(PHYS):
            at = (v * PHYS + s) * ROWS
            both = jnp.concatenate([one[at : at + ROWS, :] for one in results], axis=0)
            both = both.astype(jnp.bfloat16)
            part = width // parts
            for p in range(parts):
                start = (p * MPOB + v) * part
                mixture_ref[s, :, start : start + part] = both[:, p * part : (p + 1) * part]


def mixed(projected, coupling, parts):
    own_rows, width = projected.shape[1], projected.shape[2] // PHYS
    side = MPOB * PHYS * ROWS
    diagonal = jnp.eye(ROWS, dtype=coupling.dtype)
    turned = jnp.transpose(coupling, (1, 2, 0, 3))
    spread = turned[:, :, None, :, :, None] * diagonal[None, None, :, None, None, :]
    return pl.pallas_call(
        functools.partial(mix_kernel, parts),
        grid=(own_rows // (2 * ROWS),),
        out_shape=jax.ShapeDtypeStruct((PHYS, own_rows, MPOB * width), jnp.bfloat16),
        in_specs=[
            pl.BlockSpec((side, side), lambda i: (0, 0)),
            pl.BlockSpec((MPOB, 2 * ROWS, PHYS * width), lambda i: (0, i, 0)),
        ],
        out_specs=pl.BlockSpec((PHYS, 2 * ROWS, MPOB * width), lambda i: (0, i, 0)),
        compiler_params=pltpu.CompilerParams(vmem_limit_bytes=40 * 2**20),
        cost_estimate=pl.CostEstimate(
            flops=4 * side * MPOB * PHYS * own_rows * width,
            bytes_accessed=6 * MPOB * PHYS * own_rows * width,
            transcendentals=0,
        ),
        name="mixed",
    )(spread.reshape(side, side), projected)


def shards(left_env, prev_left, cur_site, prev_site, hamiltonian, right_env, prev_right):
    left_now, prev_now = shifted((left_env[0], prev_left[0]), "seg", 1)
    own_rows = left_now.shape[0]
    bond_width = left_now.shape[2]
    current = lax.all_gather(cur_site[0], "bond", axis=0, tiled=True)
    left_terms = jnp.transpose(left_now, (1, 0, 2)).reshape(MPOB * own_rows, bond_width)
    projected = jnp.dot(
        left_terms,
        current.reshape(bond_width, PHYS * bond_width),
        preferred_element_type=jnp.float32,
    ).reshape(MPOB, own_rows, PHYS * bond_width)
    parts = lax.axis_size("bond") if own_rows % 128 == 0 else 1
    mixture = mixed(projected, hamiltonian[0], parts)
    partial_value = jnp.einsum(
        "ab,bsc->asc", prev_now, prev_site[0], preferred_element_type=jnp.float32
    ).astype(jnp.bfloat16)
    second = jnp.einsum(
        "akc,cy->kay",
        lax.all_to_all(partial_value, "bond", split_axis=0, concat_axis=2, tiled=True),
        prev_right[0],
        preferred_element_type=jnp.float32,
    )
    flat_rows = own_rows * PHYS
    right_terms = jnp.transpose(right_env[0], (1, 0, 2))
    if parts > 1:
        right = lax.all_gather(
            right_terms.reshape(MPOB * own_rows, bond_width), "bond", axis=0, tiled=True
        )
    else:
        right = lax.all_gather(right_terms, "bond", axis=1, tiled=True)
    applied = jnp.dot(
        mixture.reshape(flat_rows, MPOB * bond_width),
        right.reshape(MPOB * bond_width, bond_width),
        preferred_element_type=jnp.float32,
    )
    target = 2.0 * applied - second.reshape(flat_rows, bond_width)
    strips = [
        jnp.dot(
            target[:, start : start + STRIP].T,
            target[:, start:],
            precision=lax.Precision.HIGH,
            preferred_element_type=jnp.float32,
        )
        for start in range(0, bond_width, STRIP)
    ]
    packed = summed(jnp.concatenate(strips, axis=1))
    upper, inverse = factorize(packed, bond_width)
    norming = math.sqrt(bond_width * PHYS)
    solved = lax.dot_general(
        target,
        inverse,
        (((1,), (1,)), ((), ())),
        precision=lax.Precision.HIGH,
        preferred_element_type=jnp.float32,
    )
    new_site = (solved * norming).astype(jnp.bfloat16).reshape(PHYS, own_rows, bond_width)
    new_site = jnp.transpose(new_site, (1, 0, 2))[None]
    offset = lax.axis_index("bond") * own_rows
    center = lax.dynamic_slice_in_dim(upper, offset, own_rows, 0) / norming
    return (new_site, center[None])


def solution(mesh):
    return jax.shard_map(
        shards,
        mesh=mesh,
        in_specs=(
            P("seg", "bond", None, None),
            P("seg", None, None),
            P("seg", "bond", None, None),
            P("seg", None, None, "bond"),
            P("seg", None, None, None, None),
            P("seg", "bond", None, None),
            P("seg", None, None),
        ),
        out_specs=(P("seg", "bond", None, None), P("seg", "bond", None)),
        check_vma=False,
    )
```
